32 devices in a mesh: dp: 2 (over core), ctx: 4 (over z), tp: 4 (over y, x).
Axes of the slice: x: 2, y: 2, z: 4, core: 2. Of those that a mesh axis runs over, the one named last changes fastest.
Arguments:
- inputs: float32 [6, 1024, 768], P('dp', 'ctx'), may hold values from -6 to 6
- encoder_out: bfloat16 [6, 1024, 768], P('dp', 'ctx'), may hold values from -6 to 6
- segments: int32 [6, 1024], P('dp', 'ctx'), may hold values from 0 to 2, never falling along the last dimension, each value on 1 to 512 neighbouring positions
- encoder_segments: int32 [6, 1024], P('dp', 'ctx'), may hold values from 0 to 2, never falling along the last dimension, each value on 1 to 512 neighbouring positions
- self_gain: bfloat16 [768], P(('dp', 'ctx')), may hold values from 0.5 to 1.5
- w_query: bfloat16 [768, 768], P(('dp', 'ctx'), 'tp'), may hold values from -0.0546875 to 0.0546875
- w_key: bfloat16 [768, 768], P(('dp', 'ctx'), 'tp'), may hold values from -0.21875 to 0.21875
- w_value: bfloat16 [768, 768], P(('dp', 'ctx'), 'tp'), may hold values from -0.21875 to 0.21875
- w_out: bfloat16 [768, 768], P('tp', ('dp', 'ctx')), may hold values from -1.75 to 1.75
- relative_bucket_bias: float32 [32, 12], P(None, 'tp'), may hold values from -2 to 2
- cross_gain: bfloat16 [768], P(('dp', 'ctx')), may hold values from 0.5 to 1.5
- cw_query: bfloat16 [768, 768], P(('dp', 'ctx'), 'tp'), may hold values from -0.0546875 to 0.0546875
- cw_key: bfloat16 [768, 768], P(('dp', 'ctx'), 'tp'), may hold values from -0.21875 to 0.21875
- cw_value: bfloat16 [768, 768], P(('dp', 'ctx'), 'tp'), may hold values from -0.21875 to 0.21875
- cw_out: bfloat16 [768, 768], P('tp', ('dp', 'ctx')), may hold values from -1.75 to 1.75
- ff_gain: bfloat16 [768], P(('dp', 'ctx')), may hold values from 0.5 to 1.5
- w_gate: bfloat16 [768, 2048], P(('dp', 'ctx'), 'tp'), may hold values from -0.21875 to 0.21875
- w_up: bfloat16 [768, 2048], P(('dp', 'ctx'), 'tp'), may hold values from -0.21875 to 0.21875
- w_down: bfloat16 [2048, 768], P('tp', ('dp', 'ctx')), may hold values from -0.125 to 0.125
- cotangent: float32 [6, 1024, 768], P('dp', 'ctx'), may hold values from -6 to 6
Outputs:
- outputs: float32 [6, 1024, 768], P('dp', 'ctx')
- d_inputs: float32 [6, 1024, 768], P('dp', 'ctx')
- d_encoded: float32 [6, 1024, 768], P('dp', 'ctx')
- d_self_gain: float32 [768], P(('dp', 'ctx'))
- d_w_query: float32 [768, 768], P(('dp', 'ctx'), 'tp')
- d_w_key: float32 [768, 768], P(('dp', 'ctx'), 'tp')
- d_w_value: float32 [768, 768], P(('dp', 'ctx'), 'tp')
- d_w_out: float32 [768, 768], P('tp', ('dp', 'ctx'))
- d_rel_bias: float32 [32, 12], P(None, 'tp')
- d_cross_gain: float32 [768], P(('dp', 'ctx'))
- d_cw_query: float32 [768, 768], P(('dp', 'ctx'), 'tp')
- d_cw_key: float32 [768, 768], P(('dp', 'ctx'), 'tp')
- d_cw_value: float32 [768, 768], P(('dp', 'ctx'), 'tp')
- d_cw_out: float32 [768, 768], P('tp', ('dp', 'ctx'))
- d_ff_gain: float32 [768], P(('dp', 'ctx'))
- d_w_gate: float32 [768, 2048], P(('dp', 'ctx'), 'tp')
- d_w_up: float32 [768, 2048], P(('dp', 'ctx'), 'tp')
- d_w_down: float32 [2048, 768], P('tp', ('dp', 'ctx'))
The draws below stay inside these ranges and needn't reach their ends.
Inputs may be any that keep to these rules, and one draw needn't show every extreme that they name: `segments`: in every sequence the numbers never fall, every number 0 to 2 occurs, no document has more than 512 tokens and one has exactly that many. `encoder_segments`: in every sequence the numbers never fall, every number 0 to 2 occurs, no run has more than 512 outputs and one has exactly that many.
All inputs are finite; a program needn't handle non-finite values.
Results may differ from the reference program's by a relative error of at most 0.023.
The reference program's roundings to bfloat16 on the way count: a program that leaves them out, or rounds other values in their place, can miss the bound.
Values may be sent and summed in bfloat16 or wider, within the bound.
No kernel may reach another device: no remote copies, remote signals or barrier semaphores. Data moves between devices by JAX's collectives and lax.ppermute only.
A program may use at most 192 MiB of HBM per device.

```python
import math
from functools import partial
import jax
import jax.numpy as jnp
import numpy as np
from jax import lax

D = 768
HEADS = 12
HEAD_DIM = 64
FF = 2048
NB = 32
ELEN = 1024
LEN = 1024
NDOC = 3
DOC_MOST = 512
SEQS = 6


def block_levels(key, extent, cuts, low, top_value):
    def one(dim, blocks):
        steps = jax.random.uniform(jax.random.fold_in(jax.random.fold_in(key, 6), dim), (blocks,), jnp.float32, low / len(cuts), top_value / len(cuts))
        return jnp.repeat(jnp.exp(steps), extent[dim] // blocks).reshape((-1,) + (1,) * (len(extent) - dim - 1))

    gain = one(*cuts[0])
    for cut in cuts[1:]:
        gain = gain * one(*cut)
    return gain


def length_profile(count, total, limit, slope):
    weights = [(1 << 20) // math.isqrt(rank ** slope) + 1 for rank in range(2, count + 1)]
    rest, given = total - limit - (count - 1), [1] * (count - 1)
    while rest > 0:
        candidates = [i for i in range(count - 1) if given[i] < limit]
        pool, left = sum([weights[i] for i in candidates]), rest
        for i in candidates:
            more = min(limit - given[i], max(1, left * weights[i] // pool), rest)
            given[i] = given[i] + more
            rest = rest - more
    return np.array([limit] + given)


def ragged(key, count, total, most, slope):
    if count == 2:
        one = jax.random.randint(key, (), max(1, total - most), min(most, total - 1) + 1)
        return jnp.stack([one, total - one])
    tallies = jnp.asarray(length_profile(count, total, most, slope), jnp.int32)
    twos = (count - 1) // 2
    donor, sink = tallies[1:1 + 2 * twos:2], tallies[2:2 + 2 * twos:2]
    slack = jnp.minimum(donor - 1, most - sink)
    moved = jax.random.randint(jax.random.fold_in(key, 1), (twos,), 0, 1 << 20) % (slack + 1)
    tallies = tallies.at[1:1 + 2 * twos:2].set(donor - moved).at[2:2 + 2 * twos:2].set(sink + moved)
    return tallies[jax.random.permutation(jax.random.fold_in(key, 2), count)]


def normal_values(key, dims, scale, bound, cuts=(), held_as=jnp.bfloat16):
    factor_of = block_levels(key, dims, cuts, -0.22, 0.18) if cuts else 1.0
    drawn = jax.random.normal(key, dims, jnp.float32) * scale * factor_of
    return jnp.minimum(jnp.maximum(drawn, -bound), bound).astype(held_as)


def setup_inputs(seed: int = 0) -> dict:
    splits = jax.random.split(jax.random.key(seed), 21)
    inputs = normal_values(splits[0], (SEQS, LEN, D), 1.0, 6.0, ((0, 2), (1, 4)), jnp.float32)
    encoder_out = normal_values(splits[1], (SEQS, ELEN, D), 1.0, 6.0, ((0, 2), (1, 4)))
    segments = jax.vmap(lambda own: jnp.searchsorted(jnp.cumsum(ragged(own, NDOC, LEN, DOC_MOST, 2)), jnp.arange(LEN), side="right"))(jax.random.split(splits[2], SEQS)).reshape((SEQS, LEN)).astype(jnp.int32)
    encoder_segments = jax.vmap(lambda own: jnp.searchsorted(jnp.cumsum(ragged(own, NDOC, ELEN, ELEN // 2, 2)), jnp.arange(ELEN), side="right"))(jax.random.split(splits[3], SEQS)).reshape((SEQS, ELEN)).astype(jnp.int32)
    self_gain = jnp.clip(1.0 + 0.1 * jax.random.normal(splits[4], (D,), jnp.float32), 0.5, 1.5).astype(jnp.bfloat16)
    w_query = normal_values(splits[5], (D, HEADS * HEAD_DIM), (16 * D) ** -0.5, 0.0546875, ((0, 8), (1, 4)))
    w_key = normal_values(splits[6], (D, HEADS * HEAD_DIM), D ** -0.5, 0.21875, ((0, 8), (1, 4)))
    w_value = normal_values(splits[7], (D, HEADS * HEAD_DIM), D ** -0.5, 0.21875, ((0, 8), (1, 4)))
    w_out = normal_values(splits[8], (HEADS * HEAD_DIM, D), (HEADS * HEAD_DIM // 64) ** -0.5, 1.75, ((0, 4), (1, 8)))
    relative_bucket_bias = normal_values(splits[9], (NB, HEADS), 0.5, 2.0, ((1, 4),), jnp.float32)
    cross_gain = jnp.clip(1.0 + 0.1 * jax.random.normal(splits[10], (D,), jnp.float32), 0.5, 1.5).astype(jnp.bfloat16)
    cw_query = normal_values(splits[11], (D, HEADS * HEAD_DIM), (16 * D) ** -0.5, 0.0546875, ((0, 8), (1, 4)))
    cw_key = normal_values(splits[12], (D, HEADS * HEAD_DIM), D ** -0.5, 0.21875, ((0, 8), (1, 4)))
    cw_value = normal_values(splits[13], (D, HEADS * HEAD_DIM), D ** -0.5, 0.21875, ((0, 8), (1, 4)))
    cw_out = normal_values(splits[14], (HEADS * HEAD_DIM, D), (HEADS * HEAD_DIM // 64) ** -0.5, 1.75, ((0, 4), (1, 8)))
    ff_gain = jnp.clip(1.0 + 0.1 * jax.random.normal(splits[15], (D,), jnp.float32), 0.5, 1.5).astype(jnp.bfloat16)
    w_gate = normal_values(splits[16], (D, FF), D ** -0.5, 0.21875, ((0, 8), (1, 4)))
    w_up = normal_values(splits[17], (D, FF), D ** -0.5, 0.21875, ((0, 8), (1, 4)))
    w_down = normal_values(splits[18], (FF, D), FF ** -0.5, 0.125, ((0, 4), (1, 8)))
    cotangent = normal_values(splits[19], (SEQS, LEN, D), 1.0, 6.0, ((0, 2), (1, 4)), jnp.float32)
    return dict(inputs=inputs, encoder_out=encoder_out, segments=segments, encoder_segments=encoder_segments, self_gain=self_gain, w_query=w_query, w_key=w_key, w_value=w_value, w_out=w_out, relative_bucket_bias=relative_bucket_bias, cross_gain=cross_gain, cw_query=cw_query, cw_key=cw_key, cw_value=cw_value, cw_out=cw_out, ff_gain=ff_gain, w_gate=w_gate, w_up=w_up, w_down=w_down, cotangent=cotangent)


EPS = 1e-06
NEG = -1e+30
FULL_PRECISION = lax.Precision.HIGHEST
bucket_edges = [int(np.ceil(16.0 * 8.0 ** (slot_index / 16.0))) for slot_index in range(1, 16)]

@jax.custom_vjp
def low(v):
    return lax.optimization_barrier(v.astype(jnp.bfloat16)).astype(jnp.float32)

@jax.custom_vjp
def low_back(v):
    return v

def low_keep(v):
    return (low(v), None)

def low_pass(kept, grad):
    return (grad,)

def back_keep(v):
    return (v, None)

def back_low(kept, grad):
    return (low(grad),)
low.defvjp(low_keep, low_pass)
low_back.defvjp(back_keep, back_low)

def rms_norm(values, gain_vec):
    inv_root = lax.rsqrt(lax.optimization_barrier(jnp.mean(values * values, axis=-1, keepdims=True)) + EPS)
    return values * inv_root * gain_vec

def bucket_index(distance):
    clipped = jnp.maximum(distance, 0)
    result = jnp.minimum(clipped, 16)
    for edge_value in bucket_edges:
        result = result + (clipped >= edge_value).astype(jnp.int32)
    return result

def matmul(left_rows, weight):
    return jnp.einsum('std,dh->sth', left_rows, weight, precision=FULL_PRECISION)

def sequence_attention(query_low, key_low, value_low, seg_query, seg_key, bias_table, causal):
    length = query_low.shape[0]
    block_row_span = min(512, length)
    key_pos = jnp.arange(key_low.shape[0], dtype=jnp.int32)

    def one_block(block_index):
        row_start = (block_index * block_row_span).astype(jnp.int32)
        rows_query = lax.dynamic_slice_in_dim(query_low, row_start, block_row_span, 0)
        rows_seg = lax.dynamic_slice_in_dim(seg_query, row_start, block_row_span, 0)
        raw_scores = jnp.einsum('qhe,khe->hqk', rows_query, key_low, precision=FULL_PRECISION)
        scores = low_back(raw_scores)
        allowed = rows_seg[:, None] == seg_key[None, :]
        if causal:
            distance = (row_start + jnp.arange(block_row_span, dtype=jnp.int32))[:, None] - key_pos[None, :]
            allowed = allowed & (distance >= 0)
            scores = scores + jnp.transpose(bias_table[bucket_index(distance)], (2, 0, 1))
        masked_logits = jnp.where(allowed[None], scores, NEG)
        row_top = lax.optimization_barrier(jnp.max(masked_logits, axis=-1, keepdims=True))
        exp_scores = jnp.exp(masked_logits - row_top)
        prob_rows = exp_scores / lax.optimization_barrier(jnp.sum(exp_scores, axis=-1, keepdims=True))
        return jnp.einsum('hqk,khe->qhe', low(prob_rows), value_low, precision=FULL_PRECISION)
    blocks = lax.map(jax.checkpoint(one_block), jnp.arange(length // block_row_span, dtype=jnp.int32))
    return blocks.reshape(query_low.shape)

def layer(inputs, encoded, self_gain, w_query, w_key, w_value, w_out, relative_bucket_bias, cross_gain, cw_query, cw_key, cw_value, cw_out, ff_gain, w_gate, w_up, w_down, segments, encoder_segments):
    seq_count, length, model_width = inputs.shape
    head_count = relative_bucket_bias.shape[1]
    head_size = w_query.shape[1] // head_count
    enc_length = encoded.shape[1]
    act_one = low(rms_norm(inputs, self_gain))
    query_low = low(low_back(matmul(act_one, w_query))).reshape(seq_count, length, head_count, head_size)
    key_low = low(low_back(matmul(act_one, w_key))).reshape(seq_count, length, head_count, head_size)
    value_low = low(low_back(matmul(act_one, w_value))).reshape(seq_count, length, head_count, head_size)

    def self_part(packed):
        return sequence_attention(packed[0], packed[1], packed[2], packed[3], packed[3], relative_bucket_bias, True)
    attended = lax.map(self_part, (query_low, key_low, value_low, segments))
    att_low = low(low_back(attended.reshape(seq_count, length, head_count * head_size)))
    resid_one = inputs + low_back(matmul(att_low, w_out))
    act_two = low(rms_norm(resid_one, cross_gain))
    cquery = low(low_back(matmul(act_two, cw_query))).reshape(seq_count, length, head_count, head_size)
    ckey = low(low_back(matmul(encoded, cw_key))).reshape(seq_count, enc_length, head_count, head_size)
    cvalue = low(low_back(matmul(encoded, cw_value))).reshape(seq_count, enc_length, head_count, head_size)

    def cross_part(packed):
        return sequence_attention(packed[0], packed[1], packed[2], packed[3], packed[4], relative_bucket_bias, False)
    cattended = lax.map(cross_part, (cquery, ckey, cvalue, segments, encoder_segments))
    catt_low = low(low_back(cattended.reshape(seq_count, length, head_count * head_size)))
    resid_two = resid_one + low_back(matmul(catt_low, cw_out))
    act_three = low(rms_norm(resid_two, ff_gain))
    gate_pre = low_back(matmul(act_three, w_gate))
    up_pre = low_back(matmul(act_three, w_up))
    hidden = low(jax.nn.gelu(gate_pre, approximate=True) * up_pre)
    return resid_two + low_back(matmul(hidden, w_down))

def reference(inputs, encoder_out, segments, encoder_segments, self_gain, w_query, w_key, w_value, w_out, relative_bucket_bias, cross_gain, cw_query, cw_key, cw_value, cw_out, ff_gain, w_gate, w_up, w_down, cotangent):
    float_args = [member.astype(jnp.float32) for member in (inputs, encoder_out, self_gain, w_query, w_key, w_value, w_out, relative_bucket_bias, cross_gain, cw_query, cw_key, cw_value, cw_out, ff_gain, w_gate, w_up, w_down)]
    forward = partial(layer, segments=segments, encoder_segments=encoder_segments)
    result, pull_back = jax.vjp(forward, float_args[0], float_args[1], float_args[2], float_args[3], float_args[4], float_args[5], float_args[6], float_args[7], float_args[8], float_args[9], float_args[10], float_args[11], float_args[12], float_args[13], float_args[14], float_args[15], float_args[16])
    gradients = pull_back(cotangent.astype(jnp.float32))
    return (result, gradients[0], gradients[1], gradients[2], gradients[3], gradients[4], gradients[5], gradients[6], gradients[7], gradients[8], gradients[9], gradients[10], gradients[11], gradients[12], gradients[13], gradients[14], gradients[15], gradients[16])
```

```python
import jax
import jax.numpy as jnp
import numpy as np
from jax import lax
from jax.experimental import pallas as pl
from jax.experimental.pallas import tpu as pltpu
from jax.sharding import PartitionSpec as P

HEAD_DIM = 64
NB = 32
EPS = 1e-06
NEG = -1e30
BF = jnp.bfloat16
F32 = jnp.float32
FULL_PRECISION = lax.Precision.HIGHEST
bucket_edges = [int(np.ceil(16.0 * 8.0 ** (slot_index / 16.0))) for slot_index in range(1, 16)]
NN = (((1,), (0,)), ((), ()))
NT = (((1,), (1,)), ((), ()))
TN = (((0,), (0,)), ((), ()))
GELU_C = float(np.sqrt(2.0 / np.pi))


def bucket_index(distance):
    clipped = jnp.maximum(distance, 0)
    result = jnp.minimum(clipped, 16)
    for edge_value in bucket_edges:
        result = result + (clipped >= edge_value).astype(jnp.int32)
    return result


def mm(left, right, dims=NN):
    return lax.dot_general(left, right, dims, preferred_element_type=F32)


def run(name, body, scal, ins, outs, grid=1, scratch=(), flops=0):
    def spec(shape, kind):
        rest = (0,) * (len(shape) - 1)
        if kind == "s":
            return pl.BlockSpec((1,) + tuple(shape[1:]), lambda s, sc: (s,) + rest)
        if kind == "c":
            block = (shape[0], 1) + tuple(shape[2:])
            return pl.BlockSpec(block, lambda s, sc: (0, s) + (0,) * (len(shape) - 2))
        if isinstance(kind, int):
            return pl.BlockSpec((shape[0], kind, shape[2]), lambda s, sc: (0, sc[0], 0))
        return pl.BlockSpec(tuple(shape), lambda s, sc: (0,) + rest)

    n_in, n_out = len(ins), len(outs)

    def kernel(sc, *refs):
        body(sc, refs[:n_in], refs[n_in : n_in + n_out], refs[n_in + n_out :])

    moved = sum(int(np.prod(a.shape)) * a.dtype.itemsize for a, _ in ins)
    moved += sum(int(np.prod(s)) * jnp.dtype(d).itemsize for s, d, _ in outs)
    return pl.pallas_call(
        kernel,
        out_shape=[jax.ShapeDtypeStruct(tuple(s), d) for s, d, _ in outs],
        grid_spec=pltpu.PrefetchScalarGridSpec(
            num_scalar_prefetch=1,
            grid=(grid,),
            in_specs=[spec(a.shape, k) for a, k in ins],
            out_specs=[spec(s, k) for s, _, k in outs],
            scratch_shapes=list(scratch),
        ),
        compiler_params=pltpu.CompilerParams(dimension_semantics=("arbitrary",)),
        cost_estimate=pl.CostEstimate(flops=int(flops), bytes_accessed=moved, transcendentals=0),
        name=name,
    )(scal, *[a for a, _ in ins])


def rows_at(index, size):
    return pl.ds(pl.multiple_of(index * size, size), size)


def norm_fwd(v, gain):
    inv = lax.rsqrt(jnp.mean(v * v, axis=-1, keepdims=True) + EPS)
    return (v * inv * gain).astype(BF)


def norm_bwd(dy, v, gain):
    inv = lax.rsqrt(jnp.mean(v * v, axis=-1, keepdims=True) + EPS)
    unit = v * inv
    d_gain = jnp.sum(dy * unit, axis=0, keepdims=True)
    d_unit = dy * gain
    inner = jnp.mean(d_unit * unit, axis=-1, keepdims=True)
    return inv * (d_unit - unit * inner), d_gain


def put_pieces(sc, scratch, piece_refs, value):
    scratch[...] = value
    size = piece_refs[0].shape[1]
    for m, ref in enumerate(piece_refs):
        ref[0] = scratch[rows_at(sc[m], size), :].astype(ref.dtype)


def take_pieces(sc, scratch, piece_refs):
    size = piece_refs[0].shape[1]
    for m, ref in enumerate(piece_refs):
        scratch[rows_at(sc[m], size), :] = ref[0]


def head_lane(width):
    return lax.broadcasted_iota(jnp.int32, (1, width), 1) // HEAD_DIM


def only_head(value, lane, h):
    return jnp.where(lane == h, value, jnp.zeros_like(value))


def attend(q, k, v, p_ref, heads, bias_of, allowed):
    lane = head_lane(q.shape[1])
    out = jnp.zeros(q.shape, F32)
    for h in range(heads):
        scores = mm(only_head(q, lane, h), k, NT)
        if bias_of is not None:
            scores = scores + bias_of(h)
        scores = jnp.where(allowed, scores, NEG)
        top = jnp.max(scores, axis=-1, keepdims=True)
        e = jnp.exp(scores - top)
        prob = (e * (1.0 / jnp.sum(e, axis=-1, keepdims=True))).astype(BF)
        p_ref[0, h] = prob
        out = jnp.where(lane == h, mm(prob, v), out)
    return out


def attend_back(d_out, q, k, v, p_ref, heads, keep):
    lane = head_lane(q.shape[1])
    dq = jnp.zeros(q.shape, F32)
    dk = dv = None
    for h in range(heads):
        d_head = only_head(d_out, lane, h)
        low_p = p_ref[0, h]
        prob = low_p.astype(F32)
        d_prob = mm(d_head, v, NT)
        both = prob * d_prob
        d_score = both - prob * jnp.sum(both, axis=-1, keepdims=True)
        if keep is not None:
            keep(h, d_score)
        low = d_score.astype(BF)
        dq = jnp.where(lane == h, mm(low, k), dq)
        dk_h = mm(low, only_head(q, lane, h), TN)
        dv_h = mm(low_p, d_head, TN)
        dk = dk_h if dk is None else dk + dk_h
        dv = dv_h if dv is None else dv + dv_h
    return dq, dk, dv


def per_device(
    inputs,
    encoder_out,
    segments,
    encoder_segments,
    self_gain,
    w_query,
    w_key,
    w_value,
    w_out,
    relative_bucket_bias,
    cross_gain,
    cw_query,
    cw_key,
    cw_value,
    cw_out,
    ff_gain,
    w_gate,
    w_up,
    w_down,
    cotangent,
):
    C, TP, DP = lax.axis_size("ctx"), lax.axis_size("tp"), lax.axis_size("dp")
    c, t, d = lax.axis_index("ctx"), lax.axis_index("tp"), lax.axis_index("dp")
    S, NR, D = inputs.shape
    ER = encoder_out.shape[1]
    HD = w_query.shape[1]
    HH = HD // HEAD_DIM
    FF = w_gate.shape[1]
    QR, QE = NR // TP, ER // TP
    RQ = S * QR
    L, E = NR * C, ER * C
    G = w_query.shape[0]
    DH = D // DP
    H = min(C - 1, -(-(L // 2 - 1) // NR))
    W = (H + 1) * NR
    N = -(-(NR + W) // 128) * 128
    near = C <= 4
    scal = jnp.stack([t ^ m for m in range(TP)] + [d, (d + 1) % DP] + [(c + m) % C for m in range(min(C, 4))])
    scal = scal.astype(jnp.int32)
    I_DP, I_CTX = TP, TP + 2

    def tp_swap(x, m):
        return lax.ppermute(x, "tp", [(i, i ^ m) for i in range(TP)])

    def dp_swap(x):
        return lax.ppermute(x, "dp", [(i, (i + 1) % DP) for i in range(DP)])

    def ctx_from(x, m):
        return lax.ppermute(x, "ctx", [((i + m) % C, i) for i in range(C)])

    def ctx_to(x, m):
        return lax.ppermute(x, "ctx", [(i, (i + m) % C) for i in range(C)])

    def ctx_up(x, k):
        return lax.ppermute(x, "ctx", [(i, i + k) for i in range(C - k)])

    def ctx_down(x, k):
        return lax.ppermute(x, "ctx", [(i + k, i) for i in range(C - k)])

    def tp_gather(x):
        return [x] + [tp_swap(x, m) for m in range(1, TP)]

    def tp_exchange(pieces):
        return [pieces[0]] + [tp_swap(pieces[m], m) for m in range(1, TP)]

    gains_here = jnp.stack([self_gain, cross_gain, ff_gain]).astype(F32)
    if near:
        small = jnp.concatenate(
            [
                segments.astype(F32).reshape(-1),
                encoder_segments.astype(F32).reshape(-1),
                gains_here.reshape(-1),
            ]
        )[None]
        smalls = [small] + [ctx_from(small, m) for m in range(1, C)]
        n_seg, n_eseg = S * NR, S * ER
        segs = [v[0, :n_seg].reshape(S, NR) for v in smalls]
        esegs = [v[0, n_seg : n_seg + n_eseg].reshape(S, ER) for v in smalls]
        seg_keys = jnp.concatenate(
            [jnp.where(c >= k, segs[C - k], -1.0) for k in range(H, 0, -1)] + [segs[0]], axis=1
        )
        eseg_keys = jnp.concatenate(esegs, axis=1)
        turned = jnp.stack([v[0, n_seg + n_eseg :].reshape(3, G) for v in smalls], axis=1)
        turned = lax.dynamic_slice_in_dim(jnp.concatenate([turned, turned], axis=1), (C - c) % C, C, 1)
        turned = turned.reshape(3, C * G)
        other = dp_swap(turned)
        gains = jnp.where(
            d == 0, jnp.concatenate([turned, other], axis=1), jnp.concatenate([other, turned], axis=1)
        )
    else:
        seg_all = lax.all_gather(segments.astype(F32), "ctx", axis=1, tiled=True)
        seg_all = jnp.concatenate([jnp.full((S, H * NR), -1.0, F32), seg_all], axis=1)
        seg_keys = lax.dynamic_slice_in_dim(seg_all, c * NR, W, 1)
        eseg_keys = lax.all_gather(encoder_segments.astype(F32), "ctx", axis=1, tiled=True)
        gains = lax.all_gather(gains_here, ("dp", "ctx"), axis=1, tiled=True)
    gain_one, gain_two, gain_three = gains[0:1], gains[1:2], gains[2:3]
    seg_rows = segments.astype(F32).reshape(S, NR, 1)
    seg_keys = seg_keys.reshape(S, 1, W)
    eseg_keys = eseg_keys.reshape(S, 1, E)

    pack_one = jnp.concatenate([w_query, w_key, w_value], axis=1)
    pack_two = jnp.concatenate([w_out.T, cw_query, cw_out.T], axis=1)
    pack_kv = jnp.concatenate([cw_key, cw_value], axis=1)
    pack_ff = jnp.concatenate([w_gate, w_up, w_down.T], axis=1)

    def whole_rows(packed, widths):
        if not near:
            full = lax.all_gather(packed, ("dp", "ctx"), axis=0, tiled=True)
            edges = np.cumsum([0] + list(widths))
            return [full[:, a:b] for a, b in zip(edges[:-1], edges[1:])]
        own = [packed] + [ctx_from(packed, m) for m in range(1, C)]
        other = [dp_swap(v) for v in own]

        def body(sc, ins, outs, scratch):
            for j in range(2):
                for m in range(C):
                    block = ins[j * C + m]
                    at = pl.multiple_of(sc[I_DP + j] * DH + sc[I_CTX + m] * G, 16)
                    first = 0
                    for ref, width in zip(outs, widths):
                        ref[pl.ds(at, G), :] = block[:, first : first + width]
                        first += width

        return run(
            "weight_rows",
            body,
            scal,
            [(v, None) for v in own + other],
            [((D, width), BF, None) for width in widths],
        )

    wq, wk, wv = whole_rows(pack_one, (HD, HD, HD))

    def every_rank(packed, count):
        if not near:
            full = lax.all_gather(packed, ("dp", "ctx"), axis=0, tiled=True)
            return [[v[:, i * HD : (i + 1) * HD] for i in range(count)] for v in tp_gather(full)]
        own = [packed] + [ctx_from(packed, m) for m in range(1, C)]
        width = packed.shape[1]

        def half_body(sc, ins, outs, scratch):
            for m in range(C):
                outs[0][pl.ds(pl.multiple_of(sc[I_CTX + m] * G, 16), G), :] = ins[m][...]

        (half,) = run("half_rows", half_body, scal, [(v, None) for v in own], [((DH, width), BF, None)])
        halves = tp_gather(half)
        others = [dp_swap(v) for v in halves]

        def body(sc, ins, outs, scratch):
            for j in range(2):
                for m in range(TP):
                    at = rows_at(sc[I_DP + j], DH)
                    for i in range(count):
                        outs[m * count + i][at, :] = ins[j * TP + m][:, i * HD : (i + 1) * HD]

        flat = run(
            "rank_rows",
            body,
            scal,
            [(v, None) for v in halves + others],
            [((D, HD), BF, None)] * (TP * count),
        )
        return [flat[m * count : (m + 1) * count] for m in range(TP)]

    def pre_body(sc, ins, outs, scratch):
        outs[0][0] = norm_fwd(ins[0][0], ins[1][...])
        outs[1][0] = outs[0][0, rows_at(sc[0], QR), :]

    act_one, act_quarter = run(
        "act_one",
        pre_body,
        scal,
        [(inputs, "s"), (gain_one, None)],
        [((S, NR, D), BF, "s"), ((S, QR, D), BF, "s")],
        grid=S,
    )
    if near:
        halo, halo_at = [], []
        for k in range(1, H + 1):
            for m, piece in enumerate(tp_gather(ctx_up(act_quarter, k))):
                halo.append(piece)
                halo_at.append(((H - k) * NR, m))
    else:
        act_all = lax.all_gather(act_one, "ctx", axis=1, tiled=True)
        act_all = jnp.concatenate([jnp.zeros((S, H * NR, D), BF), act_all], axis=1)
        halo = [lax.dynamic_slice_in_dim(act_all, c * NR, H * NR, 1)]
        halo_at = [(0, None)]

    row_of = jnp.arange(N, dtype=jnp.int32)
    lane_distance = jnp.where(row_of < W, H * NR - row_of, H * NR + N - row_of)
    bucket_here = (bucket_index(lane_distance)[None] == jnp.arange(NB, dtype=jnp.int32)[:, None]).astype(F32)
    bias_lanes = jnp.einsum("bh,bn->hn", relative_bucket_bias, bucket_here, precision=FULL_PRECISION)

    n_halo = len(halo)

    def self_body(sc, ins, outs, scratch):
        act, parts = ins[0], ins[1 : 1 + n_halo]
        rq, rk, rv, seg_q, seg_k, lanes = ins[1 + n_halo :]
        q_ref, k_ref, v_ref, p_ref = outs[:4]
        window, bias, att = scratch

        @pl.when(pl.program_id(0) == 0)
        def _():
            for h in range(HH):
                line = jnp.broadcast_to(lanes[h : h + 1, :], (NR, N))
                bias[h] = pltpu.roll(line, 0, 1, stride=1, stride_axis=0)[:, :W]

        for part, (base, m) in zip(parts, halo_at):
            if m is None:
                window[base : base + part.shape[1], :] = part[0]
            else:
                at = pl.multiple_of(base + sc[m] * QR, 16)
                window[pl.ds(at, QR), :] = part[0]
        window[H * NR :, :] = act[0]
        q = mm(act[0], rq[...]).astype(BF)
        k = mm(window[...], rk[...]).astype(BF)
        v = mm(window[...], rv[...]).astype(BF)
        q_ref[0], k_ref[0], v_ref[0] = q, k, v
        ahead = lax.broadcasted_iota(jnp.int32, (NR, W), 1) - lax.broadcasted_iota(jnp.int32, (NR, W), 0)
        allowed = (ahead <= H * NR) & (seg_q[0] == seg_k[0])
        out = attend(q, k, v, p_ref, HH, lambda h: bias[h], allowed)
        put_pieces(sc, att, outs[4:], out)

    self_out = run(
        "self_attention",
        self_body,
        scal,
        [(act_one, "s")]
        + [(v, "s") for v in halo]
        + [(wq, None), (wk, None), (wv, None), (seg_rows, "s"), (seg_keys, "s"), (bias_lanes, None)],
        [((S, NR, HD), BF, "s"), ((S, W, HD), BF, "s"), ((S, W, HD), BF, "s"), ((S, HH, NR, W), BF, "s")]
        + [((S, QR, HD), BF, "s")] * TP,
        grid=S,
        scratch=[pltpu.VMEM((W, D), BF), pltpu.VMEM((HH, NR, W), F32), pltpu.VMEM((NR, HD), F32)],
        flops=2 * S * (NR * D * HD + 2 * W * D * HD + 2 * HH * NR * W * HD),
    )
    q_self, k_self, v_self, p_self = self_out[:4]
    att_ranks = [v.reshape(RQ, HD) for v in tp_exchange(self_out[4:])]

    ranks = every_rank(pack_two, 3)
    wo_ranks, cwq_ranks, co_ranks = [[r[i] for r in ranks] for i in range(3)]

    def out_body(sc, ins, outs, scratch):
        x = ins[0][...].reshape(RQ, D)
        parts, weights = ins[1 : 1 + TP], ins[1 + TP : 1 + 2 * TP]
        queries, gain = ins[1 + 2 * TP : 1 + 3 * TP], ins[-1]
        resid = x
        for part, weight in zip(parts, weights):
            resid = resid + mm(part[...], weight[...], NT)
        act = norm_fwd(resid, gain[...])
        outs[0][...], outs[1][...] = resid, act
        for ref, weight in zip(outs[2:], queries):
            ref[...] = mm(act, weight[...]).astype(BF)

    out_res = run(
        "self_out",
        out_body,
        scal,
        [(inputs, QR)] + [(v, None) for v in att_ranks + wo_ranks + cwq_ranks + [gain_two]],
        [((RQ, D), F32, None), ((RQ, D), BF, None)] + [((RQ, HD), BF, None)] * TP,
        flops=4 * RQ * D * HD * TP,
    )
    resid_one, act_two = out_res[:2]
    cq_parts = [v.reshape(S, QR, HD) for v in tp_exchange(out_res[2:])]

    cwk, cwv = whole_rows(pack_kv, (HD, HD))
    if near:
        enc_quarter = lax.dynamic_slice_in_dim(encoder_out, t * QE, QE, 1)
        far = jnp.stack([ctx_from(enc_quarter, m) for m in range(1, C)])
        enc_parts = [(v, "c") for v in tp_gather(far)]
    else:
        enc_parts = [(lax.all_gather(encoder_out, "ctx", axis=1, tiled=True), "s")]

    def ckv_body(sc, ins, outs, scratch):
        own, parts = ins[0], ins[1 : 1 + len(enc_parts)]
        rk, rv = ins[1 + len(enc_parts) :]
        window = scratch[0]
        if near:
            window[:ER, :] = own[0]
            for m in range(1, C):
                for n in range(TP):
                    at = pl.multiple_of(m * ER + sc[n] * QE, 16)
                    window[pl.ds(at, QE), :] = parts[n][m - 1, 0]
        else:
            window[...] = parts[0][0]
        outs[0][0] = mm(window[...], rk[...]).astype(BF)
        outs[1][0] = mm(window[...], rv[...]).astype(BF)

    k_cross, v_cross = run(
        "cross_keys",
        ckv_body,
        scal,
        [(encoder_out, "s")] + enc_parts + [(cwk, None), (cwv, None)],
        [((S, E, HD), BF, "s")] * 2,
        grid=S,
        scratch=[pltpu.VMEM((E, D), BF)],
        flops=4 * S * E * D * HD,
    )

    def cross_body(sc, ins, outs, scratch):
        k_ref, v_ref, seg_q, seg_k = ins[TP:]
        cq_ref, p_ref = outs[:2]
        cq, att = scratch
        take_pieces(sc, cq, ins[:TP])
        q = cq[...]
        cq_ref[0] = q
        allowed = seg_q[0] == seg_k[0]
        out = attend(q, k_ref[0], v_ref[0], p_ref, HH, None, allowed)
        put_pieces(sc, att, outs[2:], out)

    cross_out = run(
        "cross_attention",
        cross_body,
        scal,
        [(v, "s") for v in cq_parts] + [(k_cross, "s"), (v_cross, "s"), (seg_rows, "s"), (eseg_keys, "s")],
        [((S, NR, HD), BF, "s"), ((S, HH, NR, E), BF, "s")] + [((S, QR, HD), BF, "s")] * TP,
        grid=S,
        scratch=[pltpu.VMEM((NR, HD), BF), pltpu.VMEM((NR, HD), F32)],
        flops=4 * S * HH * NR * E * HD,
    )
    q_cross, p_cross = cross_out[:2]
    catt_ranks = [v.reshape(RQ, HD) for v in tp_exchange(cross_out[2:])]

    def cout_body(sc, ins, outs, scratch):
        resid = ins[0][...]
        for part, weight in zip(ins[1 : 1 + TP], ins[1 + TP : 1 + 2 * TP]):
            resid = resid + mm(part[...], weight[...], NT)
        outs[0][...] = resid
        outs[1][...] = norm_fwd(resid, ins[-1][...])

    resid_two, act_three_q = run(
        "cross_out",
        cout_body,
        scal,
        [(v, None) for v in [resid_one] + catt_ranks + co_ranks + [gain_three]],
        [((RQ, D), F32, None), ((RQ, D), BF, None)],
        flops=2 * RQ * D * HD * TP,
    )
    act_three_parts = tp_gather(act_three_q.reshape(S, QR, D))

    wg, wu, wd = whole_rows(pack_ff, (FF, FF, FF))

    def ffn_body(sc, ins, outs, scratch):
        cot, rg, ru, rd = ins[TP:]
        act_ref, hid_ref, dgu_ref = outs[:3]
        rows, total = scratch
        take_pieces(sc, rows, ins[:TP])
        act = rows[...]
        act_ref[0] = act
        gate = mm(act, rg[...])
        up = mm(act, ru[...])
        inside = jnp.tanh(GELU_C * (gate + 0.044715 * gate * gate * gate))
        half = 0.5 * (1.0 + inside)
        gelu = gate * half
        slope = half + 0.5 * gate * (1.0 - inside * inside) * (GELU_C * (1.0 + 3 * 0.044715 * gate * gate))
        hidden = (gelu * up).astype(BF)
        hid_ref[0] = hidden
        put_pieces(sc, total, outs[3 : 3 + TP], mm(hidden, rd[...], NT))
        d_hidden = mm(cot[0].astype(BF), rd[...])
        d_gate = (d_hidden * up * slope).astype(BF)
        d_up = (d_hidden * gelu).astype(BF)
        dgu_ref[0, :, :FF] = d_gate
        dgu_ref[0, :, FF:] = d_up
        put_pieces(sc, total, outs[3 + TP :], mm(d_gate, rg[...], NT) + mm(d_up, ru[...], NT))

    piece_outs = [((S, QR, D), F32, "s")] + [((S, QR, D), BF, "s")] * (TP - 1)
    ffn_out = run(
        "feed_forward",
        ffn_body,
        scal,
        [(v, "s") for v in act_three_parts] + [(cotangent, "s"), (wg, None), (wu, None), (wd, None)],
        [((S, NR, D), BF, "s"), ((S, NR, FF), BF, "s"), ((S, NR, 2 * FF), BF, "s")] + piece_outs * 2,
        grid=S,
        scratch=[pltpu.VMEM((NR, D), BF), pltpu.VMEM((NR, D), F32)],
        flops=12 * S * NR * D * FF,
    )
    act_three, hidden, d_gate_up = ffn_out[:3]
    d_act_three = [v.reshape(RQ, D) for v in tp_exchange(ffn_out[3 + TP :])]

    def mid_three_body(sc, ins, outs, scratch):
        dy = ins[0][...]
        for part in ins[1:TP]:
            dy = dy + part[...]
        resid, cot, gain = ins[TP][...], ins[TP + 1][...].reshape(RQ, D), ins[TP + 2][...]
        dv, d_gain = norm_bwd(dy, resid, gain)
        grad = cot + dv
        low = grad.astype(BF)
        outs[0][...], outs[1][...], outs[2][...] = grad, low, d_gain
        for ref, weight in zip(outs[3:], ins[TP + 3 :]):
            ref[...] = mm(low, weight[...]).astype(BF)

    mid_three = run(
        "grad_two",
        mid_three_body,
        scal,
        [(v, None) for v in d_act_three]
        + [(resid_two, None), (cotangent, QR), (gain_three, None)]
        + [(v, None) for v in co_ranks],
        [((RQ, D), F32, None), ((RQ, D), BF, None), ((1, D), F32, None)] + [((RQ, HD), BF, None)] * TP,
        flops=2 * RQ * D * HD * TP,
    )
    grad_two, g_cross, d_ff_gain = mid_three[:3]
    d_catt_parts = [v.reshape(S, QR, HD) for v in tp_exchange(mid_three[3:])]

    def cross_back_body(sc, ins, outs, scratch):
        p_ref, q_ref, k_ref, v_ref = ins[TP:]
        d_rows, dq_rows = scratch
        take_pieces(sc, d_rows, ins[:TP])
        dq, dk, dv = attend_back(d_rows[...], q_ref[0], k_ref[0], v_ref[0], p_ref, HH, None)
        put_pieces(sc, dq_rows, outs[:TP], dq)
        size = outs[TP].shape[1]
        for m, ref in enumerate(outs[TP:]):
            ref[0, :, :HD] = dk[m * size : (m + 1) * size].astype(ref.dtype)
            ref[0, :, HD:] = dv[m * size : (m + 1) * size].astype(ref.dtype)

    if near:
        dckv_outs = [((S, ER, 2 * HD), F32, "s")] + [((S, ER, 2 * HD), BF, "s")] * (C - 1)
    else:
        dckv_outs = [((S, E, 2 * HD), BF, "s")]
    cross_back = run(
        "cross_backward",
        cross_back_body,
        scal,
        [(v, "s") for v in d_catt_parts] + [(p_cross, "s"), (q_cross, "s"), (k_cross, "s"), (v_cross, "s")],
        [((S, QR, HD), BF, "s")] * TP + dckv_outs,
        grid=S,
        scratch=[pltpu.VMEM((NR, HD), BF), pltpu.VMEM((NR, HD), F32)],
        flops=8 * S * HH * NR * E * HD,
    )
    d_cq_ranks = [v.reshape(RQ, HD) for v in tp_exchange(cross_back[:TP])]

    def mid_two_body(sc, ins, outs, scratch):
        parts, queries = ins[:TP], ins[TP : 2 * TP]
        resid, before, gain = ins[2 * TP][...], ins[2 * TP + 1][...], ins[2 * TP + 2][...]
        dy = mm(parts[0][...], queries[0][...], NT)
        for part, weight in zip(parts[1:], queries[1:]):
            dy = dy + mm(part[...], weight[...], NT)
        dv, d_gain = norm_bwd(dy, resid, gain)
        grad = before + dv
        low = grad.astype(BF)
        outs[0][...], outs[1][...], outs[2][...] = grad, low, d_gain
        for ref, weight in zip(outs[3:], ins[2 * TP + 3 :]):
            ref[...] = mm(low, weight[...]).astype(BF)

    mid_two = run(
        "grad_one",
        mid_two_body,
        scal,
        [(v, None) for v in d_cq_ranks + cwq_ranks + [resid_one, grad_two, gain_two] + wo_ranks],
        [((RQ, D), F32, None), ((RQ, D), BF, None), ((1, D), F32, None)] + [((RQ, HD), BF, None)] * TP,
        flops=4 * RQ * D * HD * TP,
    )
    grad_one, g_self, d_cross_gain = mid_two[:3]
    d_att_parts = [v.reshape(S, QR, HD) for v in tp_exchange(mid_two[3:])]

    def self_back_body(sc, ins, outs, scratch):
        p_ref, q_ref, k_ref, v_ref = ins[TP:]
        d_rows, shifted = scratch

        @pl.when(pl.program_id(0) == 0)
        def _():
            shifted[...] = jnp.zeros_like(shifted)

        def keep(h, d_score):
            shifted[h, :, :W] += d_score

        take_pieces(sc, d_rows, ins[:TP])
        dq, dk, dv = attend_back(d_rows[...], q_ref[0], k_ref[0], v_ref[0], p_ref, HH, keep)
        outs[0][0] = dq.astype(BF)
        size = outs[2].shape[1]
        outs[1][0, :, :HD], outs[1][0, :, HD:] = dk[H * NR :], dv[H * NR :]
        for n, ref in enumerate(outs[2:-1]):
            ref[0, :, :HD] = dk[n * size : (n + 1) * size].astype(BF)
            ref[0, :, HD:] = dv[n * size : (n + 1) * size].astype(BF)

        @pl.when(pl.program_id(0) == S - 1)
        def _():
            for h in range(HH):
                rows, block = NR, shifted[h]
                while rows > 1:
                    rows //= 2
                    block = block[:rows] + pltpu.roll(block[rows:], N - rows, 1)
                outs[-1][h : h + 1, :] = block

    halo_outs = [((S, NR, 2 * HD), BF, "s")] * H if near else [((S, H * NR, 2 * HD), BF, "s")]
    self_back = run(
        "self_backward",
        self_back_body,
        scal,
        [(v, "s") for v in d_att_parts] + [(p_self, "s"), (q_self, "s"), (k_self, "s"), (v_self, "s")],
        [((S, NR, HD), BF, "s"), ((S, NR, 2 * HD), F32, "s")] + halo_outs + [((HH, N), F32, None)],
        grid=S,
        scratch=[pltpu.VMEM((NR, HD), BF), pltpu.VMEM((HH, NR, N), F32)],
        flops=8 * S * HH * NR * W * HD,
    )
    dq_low, dkv_own, d_lanes = self_back[0], self_back[1], self_back[-1]
    if near:
        dkv_parts = [dkv_own] + [ctx_down(self_back[2 + H - k], k) for k in range(1, H + 1)]
    else:
        window = jnp.concatenate([self_back[2], dkv_own.astype(BF)], axis=1)
        spread = jnp.zeros((S, (H + C) * NR, 2 * HD), BF)
        spread = lax.dynamic_update_slice_in_dim(spread, window, c * NR, 1)
        dkv_parts = [
            lax.psum_scatter(spread[:, H * NR :], "ctx", scatter_dimension=1, tiled=True).astype(F32)
        ]

    def act_back_body(sc, ins, outs, scratch):
        total = ins[1][0]
        for part in ins[2:-3]:
            total = total + part[0]
        low = total.astype(BF)
        outs[0][0] = low
        rq, rk, rv = ins[-3:]
        grad = mm(ins[0][0], rq[...], NT) + mm(low[:, :HD], rk[...], NT) + mm(low[:, HD:], rv[...], NT)
        put_pieces(sc, scratch[0], outs[1:], grad)

    act_back = run(
        "self_projections_back",
        act_back_body,
        scal,
        [(dq_low, "s")] + [(v, "s") for v in dkv_parts] + [(wq, None), (wk, None), (wv, None)],
        [((S, NR, 2 * HD), BF, "s")] + piece_outs,
        grid=S,
        scratch=[pltpu.VMEM((NR, D), F32)],
        flops=6 * S * NR * D * HD,
    )
    dkv_low = act_back[0]
    d_act_one = [v.reshape(RQ, D) for v in tp_exchange(act_back[1:])]

    def last_body(sc, ins, outs, scratch):
        dy = ins[0][...]
        for part in ins[1:TP]:
            dy = dy + part[...]
        dv, d_gain = norm_bwd(dy, ins[TP][...].reshape(RQ, D), ins[TP + 1][...])
        outs[0][...] = (ins[TP + 2][...] + dv).astype(BF)
        outs[1][...] = d_gain

    d_in_quarter, d_self_gain = run(
        "d_inputs_rows",
        last_body,
        scal,
        [(v, None) for v in d_act_one] + [(inputs, QR), (gain_one, None), (grad_one, None)],
        [((RQ, D), BF, None), ((1, D), F32, None)],
    )

    def spread_rows(quarter, size):
        parts = tp_gather(quarter.reshape(S, size, D))

        def body(sc, ins, outs, scratch):
            for m, ref in enumerate(ins):
                outs[0][0, rows_at(sc[m], size), :] = ref[0].astype(F32)

        return run("all_rows", body, scal, [(v, "s") for v in parts], [((S, size * TP, D), F32, "s")], grid=S)[0]

    def sum_body(sc, ins, outs, scratch):
        total = ins[0][...]
        for ref in ins[1:]:
            total = total + ref[...]
        outs[0][...] = total.astype(BF)

    out_parts = [v.reshape(RQ, D) for v in tp_exchange(ffn_out[3 : 3 + TP])]
    (out_quarter,) = run(
        "output_rows", sum_body, scal, [(v, None) for v in [resid_two] + out_parts], [((RQ, D), BF, None)]
    )
    outputs = spread_rows(out_quarter, QR)

    if near:
        dckv_parts = [cross_back[TP]] + [ctx_to(cross_back[TP + m], m) for m in range(1, C)]
    else:
        dckv_parts = [lax.psum_scatter(cross_back[TP], "ctx", scatter_dimension=1, tiled=True).astype(F32)]

    def enc_back_body(sc, ins, outs, scratch):
        total = ins[0][0]
        for part in ins[1:-2]:
            total = total + part[0]
        low = total.astype(BF)
        outs[0][0] = low
        rk, rv = ins[-2:]
        put_pieces(sc, scratch[0], outs[1:], mm(low[:, :HD], rk[...], NT) + mm(low[:, HD:], rv[...], NT))

    enc_back = run(
        "encoder_back",
        enc_back_body,
        scal,
        [(v, "s") for v in dckv_parts] + [(cwk, None), (cwv, None)],
        [((S, ER, 2 * HD), BF, "s"), ((S, QE, D), F32, "s")] + [((S, QE, D), BF, "s")] * (TP - 1),
        grid=S,
        scratch=[pltpu.VMEM((ER, D), F32)],
        flops=4 * S * ER * D * HD,
    )
    dckv_low = enc_back[0]
    enc_sum = [v.reshape(S * QE, D) for v in tp_exchange(enc_back[1:])]
    (d_enc_quarter,) = run(
        "encoder_rows", sum_body, scal, [(v, None) for v in enc_sum], [((S * QE, D), BF, None)]
    )
    d_encoded = spread_rows(d_enc_quarter, QE)
    d_inputs = spread_rows(d_in_quarter, QR)

    def over_tokens(left, right):
        left, right = left.reshape(-1, left.shape[-1]), right.reshape(-1, right.shape[-1])
        return mm(left, right, TN)

    def core_half(full):
        if not near:
            return full
        other = lax.dynamic_slice_in_dim(full, ((d + 1) % DP) * DH, DH, 0).astype(BF)
        return lax.dynamic_slice_in_dim(full, d * DH, DH, 0) + dp_swap(other)

    def owners(rows):
        if not near:
            return lax.psum_scatter(rows.astype(BF), ("dp", "ctx"), scatter_dimension=0, tiled=True).astype(F32)
        total = lax.dynamic_slice_in_dim(rows, c * G, G, 0)
        for m in range(1, C):
            piece = lax.dynamic_slice_in_dim(rows, ((c + m) % C) * G, G, 0).astype(BF)
            total = total + ctx_to(piece, m)
        return total

    dw_ff = owners(
        core_half(
            jnp.concatenate(
                [over_tokens(act_three, d_gate_up), over_tokens(cotangent.astype(BF), hidden)], axis=1
            )
        )
    )
    rank_grads = []
    for left, rights in ((g_self, att_ranks), (act_two, d_cq_ranks), (g_cross, catt_ranks)):
        rank_grads.append(core_half(over_tokens(left, jnp.concatenate(rights, axis=1))))
    pieces = [
        jnp.concatenate([v[:, m * HD : (m + 1) * HD] for v in rank_grads], axis=1) for m in range(TP)
    ]
    dw_ranks = pieces[0]
    for m in range(1, TP):
        dw_ranks = dw_ranks + tp_swap(pieces[m].astype(BF), m)
    dw_here = core_half(
        jnp.concatenate(
            [
                over_tokens(act_one, dq_low),
                over_tokens(act_one, dkv_low),
                over_tokens(encoder_out, dckv_low),
            ],
            axis=1,
        )
    )
    dw_attn = owners(jnp.concatenate([dw_ranks, dw_here], axis=1))
    d_wo, d_cwq, d_co, d_wq, d_wk, d_wv, d_cwk, d_cwv = [
        dw_attn[:, i * HD : (i + 1) * HD] for i in range(8)
    ]
    d_wg, d_wu, d_wd = [dw_ff[:, i * FF : (i + 1) * FF] for i in range(3)]

    gain_rows = jnp.concatenate([d_self_gain, d_cross_gain, d_ff_gain], axis=0)
    d_bias = jnp.einsum("hn,bn->bh", d_lanes, bucket_here, precision=FULL_PRECISION)
    if near:
        for m in (1, 2):
            if m < TP:
                gain_rows = gain_rows + tp_swap(gain_rows, m)
        flat = jnp.concatenate([gain_rows.reshape(-1), d_bias.reshape(-1)])[None]
        flat = flat + dp_swap(flat)
        for m in (1, 2):
            if m < C:
                flat = flat + lax.ppermute(flat, "ctx", [(i, i ^ m) for i in range(C)])
        gain_rows = flat[0, : 3 * D].reshape(3, D)
        d_bias = flat[0, 3 * D :].reshape(NB, HH)
    else:
        gain_rows = lax.psum(gain_rows, ("dp", "ctx", "tp"))
        d_bias = lax.psum(d_bias, ("dp", "ctx"))
    gain_rows = lax.dynamic_slice_in_dim(gain_rows, (d * C + c) * G, G, 1)

    return (
        outputs,
        d_inputs,
        d_encoded,
        gain_rows[0],
        d_wq,
        d_wk,
        d_wv,
        d_wo.T,
        d_bias,
        gain_rows[1],
        d_cwq,
        d_cwk,
        d_cwv,
        d_co.T,
        gain_rows[2],
        d_wg,
        d_wu,
        d_wd.T,
    )


def solution(mesh):
    rows, where = P("dp", "ctx", None), P("dp", "ctx")
    vec, tall, wide, buckets = P(("dp", "ctx")), P(("dp", "ctx"), "tp"), P("tp", ("dp", "ctx")), P(None, "tp")
    return jax.shard_map(
        per_device,
        mesh=mesh,
        in_specs=(
            (rows, rows, where, where, vec, tall, tall, tall, wide, buckets, vec, tall, tall, tall, wide, vec)
            + (tall, tall, wide, rows)
        ),
        out_specs=(
            (rows, rows, rows, vec, tall, tall, tall, wide, buckets, vec, tall, tall, tall, wide, vec)
            + (tall, tall, wide)
        ),
        check_vma=False,
    )
```
